128 devices in a mesh: pipe: 16 (over z, x_hi, core), dp: 8 (over x_lo, y).
Axes of the slice: x: 4 (x_hi: 2, x_lo: 2; x = x_hi * 2 + x_lo), y: 4, z: 4, core: 2. Of those that a mesh axis runs over, the one named last changes fastest.
Arguments:
- grads: bfloat16 [16, 2, 512, 8192], P('pipe', None, 'dp'), may hold values from -6 to 6
- weights: bfloat16 [16, 8192, 8192], P('pipe', 'dp'), may hold values from -0.0625 to 0.0625
- saved: bfloat16 [16, 3, 512, 8192], P('pipe', None, 'dp'), may hold values from -6 to 6
- plan: int32 [16, 2], P('pipe'), may hold values from 0 to 2, as said below
- block_of_section: int32 [16], P('pipe'), may hold values from 0 to 15, as said below
Outputs:
- upstream: bfloat16 [16, 2, 512, 8192], P('pipe', None, 'dp')
- inverse: bfloat16 [16, 512, 512], P('pipe')
The draws below stay inside these ranges and needn't reach their ends.
Inputs may be any that keep to these rules, and one draw needn't show every extreme that they name: `plan`: each row names 2 different slots. `block_of_section`: sections name distinct block numbers where 16 >= 16; otherwise every block number is named by 1 section.
All inputs are finite; a program needn't handle non-finite values.
Results may differ from the reference program's by a relative error of at most 0.001.
Values may be sent and summed in bfloat16 or wider, within the bound.
No kernel may reach another device: no remote copies, remote signals or barrier semaphores. Data moves between devices by JAX's collectives and lax.ppermute only.
A program may use at most 128 MiB of HBM per device.

```python
import jax
import jax.numpy as jnp
from jax import lax

D = 8192
BLK = 512
MB = 2
SAVED = 3
TOK = 512
N_PIPE = 16


def draw_plan(key, part):
    score_key = jax.random.fold_in(key, 11)
    row_key = jax.random.fold_in(key, 12)
    scores = jax.random.randint(score_key, (N_PIPE, SAVED), 0, 1 << 20) * SAVED + jnp.arange(SAVED, dtype=jnp.int32)[None, :]
    chosen_row = jax.random.randint(row_key, (), 0, N_PIPE)
    is_row = jnp.arange(N_PIPE, dtype=jnp.int32)[:, None] == chosen_row
    column = jnp.arange(SAVED, dtype=jnp.int32)[None, :]
    scores = jnp.where(is_row & (column == SAVED - 1), -2, scores)
    scores = jnp.where(is_row & (column == 0), -1, scores)
    order = jnp.argsort(scores, axis=1, stable=True)
    return order[:, :MB].astype(jnp.int32)


def draw_block_of_section(key, part):
    perm_key = jax.random.fold_in(key, 21)
    scores = jax.random.randint(perm_key, (N_PIPE,), 0, 1 << 20) * N_PIPE + jnp.arange(N_PIPE, dtype=jnp.int32)
    order = jnp.argsort(scores, stable=True).astype(jnp.int32)
    return order % (D // BLK)


def levels(rng, shape, pieces, low, largest):
    factor_of, own = 1.0, jax.random.fold_in(rng, 6)
    for axis_at, shards_of in pieces:
        steps = jnp.exp(jax.random.uniform(jax.random.fold_in(own, axis_at), (shards_of,), jnp.float32, low / len(pieces), largest / len(pieces)))
        factor_of = factor_of * jnp.repeat(steps, shape[axis_at] // shards_of).reshape([-1 if axis == axis_at else 1 for axis in range(len(shape))])
    return factor_of


def noise(key, dims, spread, bound, split=(), kind=jnp.bfloat16):
    factor_of = levels(key, dims, split, -0.22, 0.18) if split else 1.0
    drawn = jax.random.normal(key, dims, jnp.float32) * spread * factor_of
    return jnp.minimum(jnp.maximum(drawn, -bound), bound).astype(kind)


def setup_inputs(seed: int = 0) -> dict:
    keys = jax.random.split(jax.random.key(seed), 6)
    grads = noise(keys[0], (N_PIPE, MB, TOK, D), 1.0, 6.0, ((0, 16), (2, 8)))
    weights = noise(keys[1], (N_PIPE, D, D), D ** -0.5, 0.0625, ((0, 16), (1, 8)))
    saved = noise(keys[2], (N_PIPE, SAVED, TOK, D), 1.0, 6.0, ((0, 16), (2, 8)))
    plan = draw_plan(jax.random.fold_in(keys[5], 71), 0)
    block_of_section = draw_block_of_section(jax.random.fold_in(keys[5], 71), 0)
    return dict(grads=grads, weights=weights, saved=saved, plan=plan, block_of_section=block_of_section)


def invert_block(factor):
    lower = lax.linalg.cholesky(factor)
    eye = jnp.eye(factor.shape[0], dtype=jnp.float32)
    lower_inv = lax.linalg.triangular_solve(lower, eye, left_side=True, lower=True)
    return jnp.dot(lower_inv.T, lower_inv, precision=lax.Precision.HIGHEST).astype(jnp.bfloat16)

def one_section(packed):
    grad_section, weight_section, saved_section, slots, block = packed
    input_grad = jnp.einsum('mtd,id->mti', grad_section.astype(jnp.float32), weight_section.astype(jnp.float32)).astype(jnp.bfloat16)
    columns = lax.dynamic_slice_in_dim(saved_section, (block * BLK).astype(jnp.int32), BLK, 2)
    picked = jnp.take(columns, slots, axis=0).reshape(-1, BLK)
    gram = jnp.dot(picked.T.astype(jnp.float32), picked.astype(jnp.float32), preferred_element_type=jnp.float32)
    factor = gram / (MB * TOK) + jnp.eye(BLK, dtype=jnp.float32)
    return (input_grad, invert_block(factor))

def reference(grads, weights, saved, plan, block_of_section):
    input_grad, inverse = lax.map(one_section, (grads, weights, saved, plan, block_of_section))
    upstream = jnp.concatenate([input_grad[1:], jnp.zeros_like(input_grad[:1])], axis=0)
    return (upstream, inverse)
```

```python
import functools

import jax
import jax.numpy as jnp
from jax import lax
from jax.experimental import pallas as pl
from jax.experimental.pallas import tpu as pltpu
from jax.sharding import PartitionSpec as P

BLK = 512
PANEL = 128
HIGHEST = lax.Precision.HIGHEST

NX, NY = 2, 4


def at(x, y):
    return (x % NX) * NY + y % NY


def hop(value, dx, dy):
    pairs = [(at(x, y), at(x + dx, y + dy)) for x in range(NX) for y in range(NY)]
    return lax.ppermute(value, "dp", pairs)


def to_owner(value, dx, dy):
    sections = lax.axis_size("pipe")
    size = NX * NY
    pairs = [
        (p * size + at(x, y), (p - 1) * size + at(x + dx, y + dy))
        for p in range(1, sections)
        for x in range(NX)
        for y in range(NY)
    ]
    return lax.ppermute(value, ("pipe", "dp"), pairs)


def pick_kernel(plan_ref, block_ref, saved_ref, out_ref):
    out_ref[...] = saved_ref[...]


def pick_rows(saved, plan, block):
    _, _, tokens, _ = saved.shape
    picks = plan.shape[1]
    return pl.pallas_call(
        pick_kernel,
        out_shape=jax.ShapeDtypeStruct((picks * tokens, BLK), saved.dtype),
        grid_spec=pltpu.PrefetchScalarGridSpec(
            num_scalar_prefetch=2,
            grid=(picks,),
            in_specs=[
                pl.BlockSpec(
                    (None, None, tokens, BLK), lambda m, plan, block: (0, plan[m], 0, block[0])
                )
            ],
            out_specs=pl.BlockSpec((tokens, BLK), lambda m, plan, block: (m, 0)),
        ),
        cost_estimate=pl.CostEstimate(flops=0, bytes_accessed=4 << 20, transcendentals=0),
        name="pick_rows",
    )(plan[0], block, saved)


def factor_kernel(count, *refs):
    out_ref = refs[-1]
    total = None
    for ref in refs[:-1]:
        rows = ref[...]
        part = lax.dot_general(
            rows, rows, (((0,), (0,)), ((), ())), preferred_element_type=jnp.float32
        )
        total = part if total is None else total + part
    i = lax.broadcasted_iota(jnp.int32, (BLK, BLK), 0)
    j = lax.broadcasted_iota(jnp.int32, (BLK, BLK), 1)
    out_ref[...] = total / count + jnp.where(i == j, 1.0, 0.0)


def build_factor(rows, count):
    return pl.pallas_call(
        functools.partial(factor_kernel, count),
        out_shape=jax.ShapeDtypeStruct((BLK, BLK), jnp.float32),
        cost_estimate=pl.CostEstimate(flops=10 << 30, bytes_accessed=2 << 20, transcendentals=0),
        name="factor",
    )(*rows)


def eliminate(a):
    n = a.shape[0]
    lane = lax.broadcasted_iota(jnp.int32, (n - 8, n), 1)
    lane8 = lax.broadcasted_iota(jnp.int32, (8, n), 1)
    row8 = lax.broadcasted_iota(jnp.int32, (8, n), 0)

    def turn(_, a):
        top, rest = a[:8], a[8:]
        columns = [jnp.broadcast_to(rest[:, j : j + 1], rest.shape) for j in range(8)]
        for j in range(8):
            scale = 1.0 / top[j : j + 1, j : j + 1]
            pivot = jnp.where(lane8[:1] == j, scale, top[j : j + 1, :] * scale)
            column = jnp.where(row8 == j, -1.0, jnp.broadcast_to(top[:, j : j + 1], top.shape))
            top = jnp.where((lane8 == j) | (row8 == j), 0.0, top) - column * pivot
        rest = jnp.where(lane < 8, 0.0, rest)
        for j in range(8):
            rest = rest - columns[j] * top[j : j + 1, :]
        return pltpu.roll(jnp.concatenate([rest, top], axis=0), n - 8, axis=1)

    return lax.fori_loop(0, n // 8, turn, a)


def panel_kernel(step, a_ref, *refs):
    out_ref = refs[-1]
    panels = BLK // PANEL
    cut = [slice(i * PANEL, (i + 1) * PANEL) for i in range(panels)]
    here = cut[step]
    inverse = eliminate(a_ref[here, here])
    row = jnp.dot(inverse, a_ref[here, :], precision=HIGHEST, preferred_element_type=jnp.float32)
    row = jnp.concatenate(
        [inverse if i == step else row[:, cut[i]] for i in range(panels)], axis=1
    )
    for i in range(panels):
        if i == step:
            out_ref[here, :] = row.astype(out_ref.dtype)
            continue
        base = jnp.concatenate(
            [
                jnp.zeros((PANEL, PANEL), jnp.float32) if c == step else a_ref[cut[i], cut[c]]
                for c in range(panels)
            ],
            axis=1,
        )
        change = jnp.dot(
            a_ref[cut[i], here], row, precision=HIGHEST, preferred_element_type=jnp.float32
        )
        out_ref[cut[i], :] = (base - change).astype(out_ref.dtype)


def invert_panel(a, step, after=()):
    last = step == BLK // PANEL - 1
    return pl.pallas_call(
        functools.partial(panel_kernel, step),
        out_shape=jax.ShapeDtypeStruct((BLK, BLK), jnp.bfloat16 if last else jnp.float32),
        in_specs=[pl.BlockSpec(memory_space=pltpu.VMEM)]
        + [pl.BlockSpec(memory_space=pl.ANY)] * len(after),
        out_specs=pl.BlockSpec(memory_space=pltpu.VMEM),
        cost_estimate=pl.CostEstimate(flops=12 << 30, bytes_accessed=2 << 20, transcendentals=0),
        name=f"panel{step}",
    )(a, *after)


def product_kernel(counts, x_refs, w_ref, out_refs):
    x = jnp.concatenate([ref[...] for ref in x_refs], axis=0)
    y = lax.dot_general(
        x, w_ref[...], (((1,), (1,)), ((), ())), preferred_element_type=jnp.float32
    )
    start = 0
    for ref in out_refs:
        rows = ref.shape[0]
        ref[...] = y[start : start + rows].astype(ref.dtype)
        start += rows


def products(shards, weight, name, width=256, after=()):
    depth = weight.shape[1]
    pieces = [piece for shard in shards for piece in shard]
    sizes = [sum(piece.shape[0] for piece in shard) for shard in shards]
    n, extra, total = len(pieces), len(after), sum(sizes)

    def kernel(*refs):
        product_kernel(sizes, refs[:n], refs[n], refs[n + 1 + extra :])

    return pl.pallas_call(
        kernel,
        out_shape=[jax.ShapeDtypeStruct((s, weight.shape[0]), weight.dtype) for s in sizes],
        grid=(weight.shape[0] // width,),
        in_specs=[pl.BlockSpec(p.shape, lambda i: (0, 0)) for p in pieces]
        + [pl.BlockSpec((width, depth), lambda i: (i, 0))]
        + [pl.BlockSpec(memory_space=pl.ANY)] * extra,
        out_specs=[pl.BlockSpec((s, width), lambda i: (0, i)) for s in sizes],
        compiler_params=pltpu.CompilerParams(vmem_limit_bytes=48 << 20),
        cost_estimate=pl.CostEstimate(
            flops=2 * total * depth * weight.shape[0],
            bytes_accessed=2 * depth * (total + weight.shape[0]),
            transcendentals=0,
        ),
        name=name,
    )(*pieces, weight, *after)


def collect_kernel(offsets, *refs):
    parts, out_ref, sem = refs[:-2], refs[-2], refs[-1]
    width = parts[0].shape[1]
    me = lax.axis_index("dp")
    x, y = me // NY, me % NY
    copies = []
    for i, (part, (dx, dy)) in enumerate(zip(parts, offsets)):
        source = (x + NX - dx) % NX * NY + (y + NY - dy) % NY
        start = pl.multiple_of(source * width, width)
        copies.append(
            pltpu.make_async_copy(part, out_ref.at[:, pl.ds(start, width)], sem.at[i])
        )
    for copy in copies:
        copy.start()
    for copy in copies:
        copy.wait()


def collect(parts, offsets):
    rows, width = parts[0].shape
    return pl.pallas_call(
        functools.partial(collect_kernel, offsets),
        out_shape=jax.ShapeDtypeStruct((rows, width * len(parts)), parts[0].dtype),
        in_specs=[pl.BlockSpec(memory_space=pl.ANY)] * len(parts),
        out_specs=pl.BlockSpec(memory_space=pltpu.VMEM),
        scratch_shapes=[pltpu.SemaphoreType.DMA((len(parts),))],
        cost_estimate=pl.CostEstimate(flops=0, bytes_accessed=4 << 20, transcendentals=0),
        name="collect",
    )(*parts)


def on_device(grads, weights, saved, plan, block_of_section):
    weight = weights[0]
    _, batches, tokens, depth = grads.shape
    m0, m1 = grads[0, 0], grads[0, 1]

    up1, down1, over0 = hop(m1, 0, 1), hop(m1, 0, -1), hop(m0, 1, 0)
    mine = pick_rows(saved, plan, block_of_section)
    others = [
        hop(mine, dx, dy) for dx in range(NX) for dy in range(NY) if (dx, dy) != (0, 0)
    ]
    up0, down0, over1 = hop(m0, 0, 1), hop(m0, 0, -1), hop(m1, 1, 0)
    factor = build_factor([mine, *others], batches * tokens * NX * NY)
    inverse = invert_panel(factor, 0)

    side_up0 = hop(over0, 0, 1)
    two1 = hop(down1, 0, -1)
    side_up1 = hop(up1, 1, 0)
    inverse = invert_panel(inverse, 1)

    two0 = hop(up0, 0, 1)
    side_down1 = hop(over1, 0, -1)
    side_down0 = hop(down0, 1, 0)

    first = products(
        [[m0, m1], [up0, up1], [down0, down1], [over0, over1]], weight, "product_a"
    )
    offsets = [(0, 0), (0, -1), (0, 1), (1, 0)]
    results = [to_owner(v, *o) for v, o in zip(first, offsets)]
    inverse = invert_panel(inverse, 2)

    cut = tokens // 4
    far_a = hop(side_up0[: tokens - cut], 0, 1)
    far_c = hop(two1[:cut], 1, 0)
    far_b = hop(two0[tokens - cut :], 1, 0)
    far_d = hop(side_down1[cut:], 0, -1)
    inverse = invert_panel(inverse, 3)

    second = products(
        [[two0, two1], [side_up0, side_up1], [side_down0, side_down1]], weight, "product_b"
    )
    more = [(0, 2), (1, -1), (1, 1)]
    results += [to_owner(v, *o) for v, o in zip(second, more)]
    offsets += more

    (last,) = products([[far_a, far_b, far_c, far_d]], weight, "product_c")
    results.append(to_owner(last, 1, 2))
    offsets.append((1, 2))

    upstream = collect(results, offsets)
    return (upstream.reshape(1, batches, tokens, depth), inverse[None])


def solution(mesh):
    in_specs = (
        P("pipe", None, "dp", None),
        P("pipe", "dp", None),
        P("pipe", None, "dp", None),
        P("pipe", None),
        P("pipe"),
    )
    out_specs = (P("pipe", None, "dp", None), P("pipe", None, None))
    return jax.shard_map(
        on_device, mesh=mesh, in_specs=in_specs, out_specs=out_specs, check_vma=False
    )
```

```python
import functools

import jax
import jax.numpy as jnp
from jax import lax
from jax.experimental import pallas as pl
from jax.experimental.pallas import tpu as pltpu
from jax.sharding import PartitionSpec as P


BLK = 512
PANEL = 128
HIGHEST = lax.Precision.HIGHEST
SMALL_VMEM = 16 << 20

NX, NY = 2, 4


def at(x, y):
    return (x % NX) * NY + y % NY


def hop(value, dx, dy):
    pairs = [(at(x, y), at(x + dx, y + dy)) for x in range(NX) for y in range(NY)]
    return lax.ppermute(value, "dp", pairs)


def to_owner(value, dx, dy):
    sections = lax.axis_size("pipe")
    size = NX * NY
    pairs = [
        (p * size + at(x, y), (p - 1) * size + at(x + dx, y + dy))
        for p in range(1, sections)
        for x in range(NX)
        for y in range(NY)
    ]
    return lax.ppermute(value, ("pipe", "dp"), pairs)


def pick_kernel(plan_ref, block_ref, saved_ref, out_ref):
    out_ref[...] = saved_ref[...]


def pick_rows(saved, plan, block):
    _, _, tokens, _ = saved.shape
    picks = plan.shape[1]
    return pl.pallas_call(
        pick_kernel,
        out_shape=jax.ShapeDtypeStruct((picks * tokens, BLK), saved.dtype),
        grid_spec=pltpu.PrefetchScalarGridSpec(
            num_scalar_prefetch=2,
            grid=(picks,),
            in_specs=[
                pl.BlockSpec(
                    (None, None, tokens, BLK), lambda m, plan, block: (0, plan[m], 0, block[0])
                )
            ],
            out_specs=pl.BlockSpec((tokens, BLK), lambda m, plan, block: (m, 0)),
        ),
        cost_estimate=pl.CostEstimate(flops=0, bytes_accessed=4 << 20, transcendentals=0),
        name="pick_rows",
    )(plan[0], block, saved)


def eliminate(a):
    n = a.shape[0]
    lane = lax.broadcasted_iota(jnp.int32, (n - 8, n), 1)
    lane8 = lax.broadcasted_iota(jnp.int32, (8, n), 1)
    row8 = lax.broadcasted_iota(jnp.int32, (8, n), 0)

    def spread(row):
        return jnp.broadcast_to(row, (8, n))

    def turn(_, a):
        top, rest = a[:8], a[8:]
        columns = [jnp.broadcast_to(rest[:, j : j + 1], rest.shape) for j in range(8)]
        block = [jnp.broadcast_to(top[:, k : k + 1], top.shape) for k in range(8)]
        for j in range(8):
            pivot_row = [spread(column[j : j + 1]) for column in block]
            here = row8 == j
            factor = jnp.where(here, -1.0, block[j]) * (1.0 / pivot_row[j])
            for k in range(8):
                if k != j:
                    block[k] = jnp.where(here, 0.0, block[k]) - factor * pivot_row[k]
            block[j] = -factor
        terms = [block[k] * spread(top[k : k + 1]) for k in range(8)]
        while len(terms) > 1:
            terms = [u + v for u, v in zip(terms[::2], terms[1::2])]
        rows = terms[0]
        for k in range(8):
            rows = jnp.where(lane8 == k, block[k], rows)
        rest = jnp.where(lane < 8, 0.0, rest)
        for j in range(8):
            rest = rest - columns[j] * rows[j : j + 1]
        return pltpu.roll(jnp.concatenate([rest, rows], axis=0), n - 8, axis=1)

    return lax.fori_loop(0, n // 8, turn, a)


def eliminate_panel(a_ref, step, out_ref):
    panels = BLK // PANEL
    cut = [slice(i * PANEL, (i + 1) * PANEL) for i in range(panels)]
    here = cut[step]
    inverse = eliminate(a_ref[here, here])
    row = jnp.dot(inverse, a_ref[here, :], precision=HIGHEST, preferred_element_type=jnp.float32)
    row = jnp.concatenate(
        [inverse if i == step else row[:, cut[i]] for i in range(panels)], axis=1
    )
    for i in range(panels):
        if i == step:
            continue
        base = jnp.concatenate(
            [
                jnp.zeros((PANEL, PANEL), jnp.float32) if c == step else a_ref[cut[i], cut[c]]
                for c in range(panels)
            ],
            axis=1,
        )
        change = jnp.dot(
            a_ref[cut[i], here], row, precision=HIGHEST, preferred_element_type=jnp.float32
        )
        out_ref[cut[i], :] = (base - change).astype(out_ref.dtype)
    out_ref[here, :] = row.astype(out_ref.dtype)


def first_half_kernel(count, *refs):
    out_ref = refs[-1]
    total = None
    for ref in refs[:-1]:
        rows = ref[...]
        part = lax.dot_general(
            rows, rows, (((0,), (0,)), ((), ())), preferred_element_type=jnp.float32
        )
        total = part if total is None else total + part
    i = lax.broadcasted_iota(jnp.int32, (BLK, BLK), 0)
    j = lax.broadcasted_iota(jnp.int32, (BLK, BLK), 1)
    out_ref[...] = total / count + jnp.where(i == j, 1.0, 0.0)
    for step in range(BLK // PANEL // 2):
        eliminate_panel(out_ref, step, out_ref)


def second_half_kernel(a_ref, out_ref, work_ref):
    steps = list(range(BLK // PANEL // 2, BLK // PANEL))
    source = a_ref
    for step in steps[:-1]:
        eliminate_panel(source, step, work_ref)
        source = work_ref
    eliminate_panel(source, steps[-1], out_ref)


def first_half(rows, count):
    return pl.pallas_call(
        functools.partial(first_half_kernel, count),
        out_shape=jax.ShapeDtypeStruct((BLK, BLK), jnp.float32),
        in_specs=[pl.BlockSpec(memory_space=pltpu.VMEM)] * len(rows),
        out_specs=pl.BlockSpec(memory_space=pltpu.VMEM),
        cost_estimate=pl.CostEstimate(flops=16 << 30, bytes_accessed=2 << 20, transcendentals=0),
        compiler_params=pltpu.CompilerParams(vmem_limit_bytes=SMALL_VMEM),
        name="first_half",
    )(*rows)


def second_half(a):
    return pl.pallas_call(
        second_half_kernel,
        out_shape=jax.ShapeDtypeStruct((BLK, BLK), jnp.bfloat16),
        in_specs=[pl.BlockSpec(memory_space=pltpu.VMEM)],
        out_specs=pl.BlockSpec(memory_space=pltpu.VMEM),
        scratch_shapes=[pltpu.VMEM((BLK, BLK), jnp.float32)],
        cost_estimate=pl.CostEstimate(flops=16 << 30, bytes_accessed=2 << 20, transcendentals=0),
        compiler_params=pltpu.CompilerParams(vmem_limit_bytes=SMALL_VMEM),
        name="second_half",
    )(a)


def product_kernel(x_refs, w_ref, out_refs):
    x = jnp.concatenate([ref[...] for ref in x_refs], axis=0)
    y = lax.dot_general(
        x, w_ref[...], (((1,), (1,)), ((), ())), preferred_element_type=jnp.float32
    )
    start = 0
    for ref in out_refs:
        rows = ref.shape[0]
        ref[...] = y[start : start + rows].astype(ref.dtype)
        start += rows


def products(shards, weight, width=256):
    depth = weight.shape[1]
    pieces = [piece for shard in shards for piece in shard]
    sizes = [sum(piece.shape[0] for piece in shard) for shard in shards]
    n, total = len(pieces), sum(sizes)

    def kernel(*refs):
        product_kernel(refs[:n], refs[n], refs[n + 1 :])

    return pl.pallas_call(
        kernel,
        out_shape=[pltpu.HBM((s, weight.shape[0]), weight.dtype) for s in sizes],
        grid=(weight.shape[0] // width,),
        in_specs=[pl.BlockSpec(p.shape, lambda i: (0, 0)) for p in pieces]
        + [pl.BlockSpec((width, depth), lambda i: (i, 0))],
        out_specs=[pl.BlockSpec((s, width), lambda i: (0, i)) for s in sizes],
        compiler_params=pltpu.CompilerParams(vmem_limit_bytes=48 << 20),
        cost_estimate=pl.CostEstimate(
            flops=2 * total * depth * weight.shape[0],
            bytes_accessed=2 * depth * (total + weight.shape[0]),
            transcendentals=0,
        ),
    )(*pieces, weight)


def strip(out_ref, offset, width):
    dx, dy = offset
    me = lax.axis_index("dp")
    x, y = me // NY, me % NY
    source = (x + NX - dx) % NX * NY + (y + NY - dy) % NY
    return out_ref.at[:, pl.ds(pl.multiple_of(source * width, width), width)]


def collect_kernel(offsets, *refs):
    n = len(offsets)
    parts, out_ref, sem = refs[:n], refs[-2], refs[-1]
    copies = [
        pltpu.make_async_copy(part, strip(out_ref, offset, part.shape[1]), sem.at[i])
        for i, (part, offset) in enumerate(zip(parts, offsets))
    ]
    for copy in copies:
        copy.start()
    for copy in copies:
        copy.wait()


def collect(parts, offsets):
    rows, width = parts[0].shape
    return pl.pallas_call(
        functools.partial(collect_kernel, offsets),
        out_shape=pltpu.HBM((rows, width * NX * NY), parts[0].dtype),
        in_specs=[pl.BlockSpec(memory_space=pltpu.HBM)] * len(parts),
        out_specs=pl.BlockSpec(memory_space=pltpu.VMEM),
        scratch_shapes=[pltpu.SemaphoreType.DMA((len(parts),))],
        cost_estimate=pl.CostEstimate(flops=0, bytes_accessed=4 << 20, transcendentals=0),
        compiler_params=pltpu.CompilerParams(vmem_limit_bytes=SMALL_VMEM),
        name="collect",
    )(*parts)


def add_last_kernel(offset, part_ref, old_ref, out_ref, sem):
    copy = pltpu.make_async_copy(part_ref, strip(out_ref, offset, part_ref.shape[1]), sem)
    copy.start()
    copy.wait()


def add_last(part, whole, offset):
    return pl.pallas_call(
        functools.partial(add_last_kernel, offset),
        out_shape=pltpu.HBM(whole.shape, whole.dtype),
        in_specs=[
            pl.BlockSpec(memory_space=pltpu.VMEM),
            pl.BlockSpec(memory_space=pltpu.HBM),
        ],
        out_specs=pl.BlockSpec(memory_space=pltpu.HBM),
        scratch_shapes=[pltpu.SemaphoreType.DMA],
        input_output_aliases={1: 0},
        cost_estimate=pl.CostEstimate(flops=0, bytes_accessed=1 << 19, transcendentals=0),
        compiler_params=pltpu.CompilerParams(vmem_limit_bytes=SMALL_VMEM),
        name="add_last",
    )(part, whole)


def on_device(grads, weights, saved, plan, block_of_section):
    weight = weights[0]
    _, batches, tokens, depth = grads.shape
    m0, m1 = grads[0, 0], grads[0, 1]

    up1, down1 = hop(m1, 0, 1), hop(m1, 0, -1)
    over0 = hop(m0, 1, 0)
    mine = pick_rows(saved, plan, block_of_section)
    pair = jnp.concatenate([mine, hop(mine, 1, 0)], axis=0)
    others = [hop(pair, 0, dy) for dy in (1, -1, 2)]
    up0, down0 = hop(m0, 0, 1), hop(m0, 0, -1)
    over1 = hop(m1, 1, 0)
    (own,) = products([[m0, m1]], weight)
    inverse = second_half(first_half([pair, *others], batches * tokens * NX * NY))

    side_up0 = hop(over0, 0, 1)
    side_up1 = hop(up1, 1, 0)
    side_down0 = hop(down0, 1, 0)
    side_down1 = hop(over1, 0, -1)
    two0, two1 = hop(up0, 0, 1), hop(down1, 0, -1)
    half = tokens // 2
    far_up = hop(side_up0[:half], 0, 1)
    far_down = hop(side_down0[half:], 0, -1)
    far_over = hop(two1, 1, 0)

    near = products([[up0, up1], [down0, down1], [over0, over1]], weight)
    next_near = products([[two0, two1], [side_up0, side_up1], [side_down0, side_down1]], weight)
    far = products([[far_up, far_down, far_over]], weight)
    offsets = [(0, 0), (0, -1), (0, 1), (1, 0), (0, 2), (1, -1), (1, 1), (1, 2)]
    results = [
        to_owner(value, *offset)
        for value, offset in zip([own, *near, *next_near, *far], offsets)
    ]
    upstream = add_last(results[-1], collect(results[:-1], offsets[:-1]), offsets[-1])
    return (upstream.reshape(1, batches, tokens, depth), inverse[None])


def solution(mesh):
    in_specs = (
        P("pipe", None, "dp", None),
        P("pipe", "dp", None),
        P("pipe", None, "dp", None),
        P("pipe", None),
        P("pipe"),
    )
    out_specs = (P("pipe", None, "dp", None), P("pipe", None, None))
    return jax.shard_map(
        on_device, mesh=mesh, in_specs=in_specs, out_specs=out_specs, check_vma=False
    )
```

```python
import functools

import jax
import jax.numpy as jnp
from jax import lax
from jax.experimental import pallas as pl
from jax.experimental.pallas import tpu as pltpu
from jax.sharding import PartitionSpec as P


BLK = 512
PANEL = 128
HIGHEST = lax.Precision.HIGHEST
SMALL_VMEM = 16 << 20

NX, NY = 2, 4


def at(x, y):
    return (x % NX) * NY + y % NY


def hop(value, dx, dy):
    pairs = [(at(x, y), at(x + dx, y + dy)) for x in range(NX) for y in range(NY)]
    return lax.ppermute(value, "dp", pairs)


def to_owner(value, dx, dy):
    sections = lax.axis_size("pipe")
    size = NX * NY
    pairs = [
        (p * size + at(x, y), (p - 1) * size + at(x + dx, y + dy))
        for p in range(1, sections)
        for x in range(NX)
        for y in range(NY)
    ]
    return lax.ppermute(value, ("pipe", "dp"), pairs)


def pick_kernel(plan_ref, block_ref, saved_ref, out_ref):
    out_ref[...] = saved_ref[...]


def pick_rows(saved, plan, block):
    _, _, tokens, _ = saved.shape
    picks = plan.shape[1]
    return pl.pallas_call(
        pick_kernel,
        out_shape=jax.ShapeDtypeStruct((picks * tokens, BLK), saved.dtype),
        grid_spec=pltpu.PrefetchScalarGridSpec(
            num_scalar_prefetch=2,
            grid=(picks,),
            in_specs=[
                pl.BlockSpec(
                    (None, None, tokens, BLK), lambda m, plan, block: (0, plan[m], 0, block[0])
                )
            ],
            out_specs=pl.BlockSpec((tokens, BLK), lambda m, plan, block: (m, 0)),
        ),
        cost_estimate=pl.CostEstimate(flops=0, bytes_accessed=4 << 20, transcendentals=0),
        name="pick_rows",
    )(plan[0], block, saved)


def eliminate(a):
    n = a.shape[0]
    lane = lax.broadcasted_iota(jnp.int32, (n - 8, n), 1)
    lane8 = lax.broadcasted_iota(jnp.int32, (8, n), 1)
    row8 = lax.broadcasted_iota(jnp.int32, (8, n), 0)

    def spread(row):
        return jnp.broadcast_to(row, (8, n))

    def turn(_, a):
        top, rest = a[:8], a[8:]
        columns = [jnp.broadcast_to(rest[:, j : j + 1], rest.shape) for j in range(8)]
        block = [jnp.broadcast_to(top[:, k : k + 1], top.shape) for k in range(8)]
        for j in range(8):
            pivot_row = [spread(column[j : j + 1]) for column in block]
            here = row8 == j
            factor = jnp.where(here, -1.0, block[j]) * (1.0 / pivot_row[j])
            for k in range(8):
                if k != j:
                    block[k] = jnp.where(here, 0.0, block[k]) - factor * pivot_row[k]
            block[j] = -factor
        terms = [block[k] * spread(top[k : k + 1]) for k in range(8)]
        while len(terms) > 1:
            terms = [u + v for u, v in zip(terms[::2], terms[1::2])]
        rows = terms[0]
        for k in range(8):
            rows = jnp.where(lane8 == k, block[k], rows)
        rest = jnp.where(lane < 8, 0.0, rest)
        for j in range(8):
            rest = rest - columns[j] * rows[j : j + 1]
        return pltpu.roll(jnp.concatenate([rest, rows], axis=0), n - 8, axis=1)

    return lax.fori_loop(0, n // 8, turn, a)


def eliminate_panel(a_ref, step, out_ref):
    panels = BLK // PANEL
    cut = [slice(i * PANEL, (i + 1) * PANEL) for i in range(panels)]
    here = cut[step]
    inverse = eliminate(a_ref[here, here])
    row = jnp.dot(inverse, a_ref[here, :], precision=HIGHEST, preferred_element_type=jnp.float32)
    row = jnp.concatenate(
        [inverse if i == step else row[:, cut[i]] for i in range(panels)], axis=1
    )
    for i in range(panels):
        if i == step:
            continue
        base = jnp.concatenate(
            [
                jnp.zeros((PANEL, PANEL), jnp.float32) if c == step else a_ref[cut[i], cut[c]]
                for c in range(panels)
            ],
            axis=1,
        )
        change = jnp.dot(
            a_ref[cut[i], here], row, precision=HIGHEST, preferred_element_type=jnp.float32
        )
        out_ref[cut[i], :] = (base - change).astype(out_ref.dtype)
    out_ref[here, :] = row.astype(out_ref.dtype)


def inverse_kernel(count, *refs):
    *row_refs, out_ref, work_ref = refs
    total = None
    for ref in row_refs:
        rows = ref[...]
        part = lax.dot_general(
            rows, rows, (((0,), (0,)), ((), ())), preferred_element_type=jnp.float32
        )
        total = part if total is None else total + part
    i = lax.broadcasted_iota(jnp.int32, (BLK, BLK), 0)
    j = lax.broadcasted_iota(jnp.int32, (BLK, BLK), 1)
    work_ref[...] = total / count + jnp.where(i == j, 1.0, 0.0)
    last = BLK // PANEL - 1
    for step in range(last):
        eliminate_panel(work_ref, step, work_ref)
    eliminate_panel(work_ref, last, out_ref)


def factor_inverse(rows, count):
    return pl.pallas_call(
        functools.partial(inverse_kernel, count),
        out_shape=jax.ShapeDtypeStruct((BLK, BLK), jnp.bfloat16),
        in_specs=[pl.BlockSpec(memory_space=pltpu.VMEM)] * len(rows),
        out_specs=pl.BlockSpec(memory_space=pltpu.VMEM),
        scratch_shapes=[pltpu.VMEM((BLK, BLK), jnp.float32)],
        cost_estimate=pl.CostEstimate(flops=32 << 30, bytes_accessed=2 << 20, transcendentals=0),
        compiler_params=pltpu.CompilerParams(vmem_limit_bytes=SMALL_VMEM),
        name="inverse",
    )(*rows)


def products(shards, weight, width, resident=True):
    depth = weight.shape[1]
    pieces = [piece for shard in shards for piece in shard]
    sizes = [sum(piece.shape[0] for piece in shard) for shard in shards]
    n, total = len(pieces), sum(sizes)
    swap = resident and total <= 128

    def kernel(*refs):
        x = jnp.concatenate([ref[...] for ref in refs[:n]], axis=0)
        here = pl.ds(pl.multiple_of(pl.program_id(0) * width, width), width)
        w = refs[n][here, :] if resident else refs[n][...]
        dims = (((1,), (1,)), ((), ()))
        if swap:
            y = lax.dot_general(w, x, dims, preferred_element_type=jnp.float32).T
        else:
            y = lax.dot_general(x, w, dims, preferred_element_type=jnp.float32)
        start = 0
        for ref in refs[n + 1 :]:
            rows = ref.shape[0]
            ref[...] = y[start : start + rows].astype(ref.dtype)
            start += rows

    return pl.pallas_call(
        kernel,
        out_shape=[pltpu.HBM((s, weight.shape[0]), weight.dtype) for s in sizes],
        grid=(weight.shape[0] // width,),
        in_specs=[
            pl.BlockSpec(p.shape, lambda i: (0, 0), pipeline_mode=pl.Buffered(1)) for p in pieces
        ]
        + [
            pl.BlockSpec(memory_space=pltpu.VMEM)
            if resident
            else pl.BlockSpec((width, depth), lambda i: (i, 0), memory_space=pltpu.VMEM)
        ],
        out_specs=[pl.BlockSpec((s, width), lambda i: (0, i)) for s in sizes],
        compiler_params=pltpu.CompilerParams(vmem_limit_bytes=24 << 20),
        cost_estimate=pl.CostEstimate(
            flops=2 * total * depth * weight.shape[0],
            bytes_accessed=2 * depth * (total + weight.shape[0]),
            transcendentals=0,
        ),
    )(*pieces, weight)


def strip(out_ref, offset, width):
    dx, dy = offset
    me = lax.axis_index("dp")
    x, y = me // NY, me % NY
    source = (x + NX - dx) % NX * NY + (y + NY - dy) % NY
    return out_ref.at[:, pl.ds(pl.multiple_of(source * width, width), width)]


def collect_kernel(offsets, *refs):
    n = len(offsets)
    parts, out_ref, sem = refs[:n], refs[-2], refs[-1]
    copies = [
        pltpu.make_async_copy(part, strip(out_ref, offset, part.shape[1]), sem.at[i])
        for i, (part, offset) in enumerate(zip(parts, offsets))
    ]
    for copy in copies:
        copy.start()
    for copy in copies:
        copy.wait()


def collect(parts, offsets):
    rows, width = parts[0].shape
    return pl.pallas_call(
        functools.partial(collect_kernel, offsets),
        out_shape=pltpu.HBM((rows, width * NX * NY), parts[0].dtype),
        in_specs=[pl.BlockSpec(memory_space=pltpu.HBM)] * len(parts),
        out_specs=pl.BlockSpec(memory_space=pltpu.VMEM),
        scratch_shapes=[pltpu.SemaphoreType.DMA((len(parts),))],
        cost_estimate=pl.CostEstimate(flops=0, bytes_accessed=4 << 20, transcendentals=0),
        compiler_params=pltpu.CompilerParams(vmem_limit_bytes=SMALL_VMEM),
        name="collect",
    )(*parts)


def add_last_kernel(offsets, *refs):
    n = len(offsets)
    parts, out_ref, sem = refs[:n], refs[-2], refs[-1]
    copies = [
        pltpu.make_async_copy(part, strip(out_ref, offset, part.shape[1]), sem.at[i])
        for i, (part, offset) in enumerate(zip(parts, offsets))
    ]
    for copy in copies:
        copy.start()
    for copy in copies:
        copy.wait()


def add_last(parts, whole, offsets):
    return pl.pallas_call(
        functools.partial(add_last_kernel, offsets),
        out_shape=pltpu.HBM(whole.shape, whole.dtype),
        in_specs=[pl.BlockSpec(memory_space=pltpu.VMEM)] * len(parts)
        + [pl.BlockSpec(memory_space=pltpu.HBM)],
        out_specs=pl.BlockSpec(memory_space=pltpu.HBM),
        scratch_shapes=[pltpu.SemaphoreType.DMA((len(parts),))],
        input_output_aliases={len(parts): 0},
        cost_estimate=pl.CostEstimate(flops=0, bytes_accessed=1 << 19, transcendentals=0),
        compiler_params=pltpu.CompilerParams(vmem_limit_bytes=SMALL_VMEM),
        name="add_last",
    )(*parts, whole)


def on_device(grads, weights, saved, plan, block_of_section):
    weight = pltpu.with_memory_space_constraint(weights[0], pltpu.HBM)
    near_weight = pltpu.with_memory_space_constraint(weights[0], pltpu.VMEM)
    _, batches, tokens, depth = grads.shape
    rows = grads.reshape(batches * tokens, depth)
    cut = 5 * rows.shape[0] // 8
    p0, p1 = rows[:cut], rows[cut:]

    up0, down0 = hop(p0, 0, 1), hop(p0, 0, -1)
    over1 = hop(p1, 1, 0)
    mine = pick_rows(saved, plan, block_of_section)
    pair = jnp.concatenate([mine, hop(mine, 1, 0)], axis=0)
    others = [hop(pair, 0, dy) for dy in (1, -1, 2)]
    up1, down1 = hop(p1, 0, 1), hop(p1, 0, -1)
    over0 = hop(p0, 1, 0)
    inverse = factor_inverse([pair, *others], batches * tokens * NX * NY)

    two0, two1 = hop(up0, 0, 1), hop(down1, 0, -1)
    side_up0, side_up1 = hop(over0, 0, 1), hop(up1, 1, 0)
    side_down0 = hop(down0, 1, 0)
    side_down1 = hop(over1, 0, -1)
    far_down, far_over = hop(side_down0, 0, -1), hop(two1, 1, 0)

    own = products([[p0, p1]], weight, 256, False)
    near = products([[up0, up1], [down0, down1], [over0, over1]], near_weight, 512)
    middle = products([[side_down0, side_down1], [two0, two1]], near_weight, 512)
    late = products([[side_up0, side_up1]], near_weight, 512)
    last = products([[far_down, far_over]], near_weight, 512)
    offsets = [(0, 0), (0, -1), (0, 1), (1, 0), (1, 1), (0, 2), (1, -1), (1, 2)]
    results = [
        to_owner(value, *offset)
        for value, offset in zip([*own, *near, *middle, *late, *last], offsets)
    ]
    upstream = add_last(results[6:], collect(results[:6], offsets[:6]), offsets[6:])
    return (upstream.reshape(1, batches, tokens, depth), inverse[None])


def solution(mesh):
    in_specs = (
        P("pipe", None, "dp", None),
        P("pipe", "dp", None),
        P("pipe", None, "dp", None),
        P("pipe", None),
        P("pipe"),
    )
    out_specs = (P("pipe", None, "dp", None), P("pipe", None, None))
    return jax.shard_map(
        on_device, mesh=mesh, in_specs=in_specs, out_specs=out_specs, check_vma=False
    )
```
